32 devices in a mesh: grp: 2 (over y), tp: 4 (over z), dp: 2 (over x), sub: 2 (over core).
Axes of the slice: x: 2, y: 2, z: 4, core: 2. Of those that a mesh axis runs over, the one named last changes fastest.
Arguments:
- hidden_in: bfloat16 [240, 26624], P(('grp', 'dp', 'sub'), 'tp'), parts along dimension 0, may hold values from -6 to 6
- out_grad: bfloat16 [240, 8192], P(('grp', 'tp'), ('dp', 'sub')), parts along dimension 0, may hold values from -6 to 6
- base_levels: bfloat16 [26624, 8192], P('tp', ('dp', 'sub')), may hold values from -1 to 1, as said below
- base_scales: bfloat16 [416, 8192], P('tp', ('dp', 'sub')), may hold values from 0.0079956055 to 0.015991211
- kron_outer: float32 [4, 4], P('tp', ('dp', 'sub')), may hold values from -3 to 3
- kron_left: bfloat16 [6656, 16], replicated, may hold values from -0.078125 to 0.078125
- kron_right: bfloat16 [16, 2048], replicated, may hold values from -0.125 to 0.125
- sparse_rows: int32 [4, 4, 8], P('tp', ('dp', 'sub')), may hold values from 0 to 51, as said below
- sparse_cols: int32 [4, 4, 8], P('tp', ('dp', 'sub')), may hold values from 0 to 15, as said below
- sparse_count: int32 [4, 4], P('tp', ('dp', 'sub')), may hold values from 1 to 8, as said below
- sparse_values: bfloat16 [4, 4, 8, 128, 128], P('tp', ('dp', 'sub')), may hold values from -0.3125 to 0.3125
Outputs:
- layer_out: bfloat16 [240, 8192], P(('grp', 'tp'), ('dp', 'sub')), parts along dimension 0
- input_grad: bfloat16 [240, 26624], P(('grp', 'dp', 'sub'), 'tp'), parts along dimension 0
- grad_outer: float32 [8, 4], P(('grp', 'tp'), ('dp', 'sub')), parts along dimension 0
- grad_left: float32 [13312, 16], P('grp'), parts along dimension 0
- grad_right: float32 [32, 2048], P('grp'), parts along dimension 0
- grad_sparse: float32 [8, 4, 8, 128, 128], P(('grp', 'tp'), ('dp', 'sub')), parts along dimension 0
The draws below stay inside these ranges and needn't reach their ends.
There are 2 independent parts, one for each index of `grp`. The reference program is written for one: setup_inputs(seed, part) draws one part's arguments, and reference() takes and returns one part's arrays. A program takes and returns all parts, laid end to end along the dimension named above; an argument that names none is the same for every part. Nothing has to cross between parts.
Inputs may be any that keep to these rules, and one draw needn't show every extreme that they name: `base_levels`: every entry is one of the 16 levels of the NF4 code. `sparse_rows`: the 8 slots of a tile name distinct blocks, with sparse_cols. `sparse_cols`: the 8 slots of a tile name distinct blocks, with sparse_rows. `sparse_count`: slots at or past the count are unused; some tile uses all 8.
All inputs are finite; a program needn't handle non-finite values.
Results may differ from the reference program's by a relative error of at most 0.014.
Values may be sent and summed in bfloat16 or wider, within the bound.
A program may use at most 320 MiB of HBM per device.

```python
import math
import jax
import jax.numpy as jnp
from jax import lax

K = 26624
D = 8192
R = 16
BLK = 128
QB = 64
MAXB = 8
TOKENS = 120
KRON_ROWS = 4
KRON_COLS = 4
KT = 6656
DS = 2048


NF4_LEVELS = [-1.0, -0.6961928009986877, -0.5250730514526367, -0.39491748809814453, -0.28444138169288635, -0.18477343022823334, -0.09105003625154495, 0.0, 0.07958029955625534, 0.16093020141124725, 0.24611230194568634, 0.33791524171829224, 0.44070982933044434, 0.5626170039176941, 0.7229568362236023, 1.0]


def draw_base_levels(key, part):
    codes = jax.random.randint(key, (K, D), 0, 16)
    table = jnp.array(NF4_LEVELS, dtype=jnp.float32)
    return jnp.take(table, codes).astype(jnp.bfloat16)


def tile_choice(tile_key):
    per_tile = KT // BLK * (DS // BLK)
    return jax.random.permutation(tile_key, per_tile)[:MAXB]


def slot_positions(key):
    tile_total = KRON_ROWS * KRON_COLS
    tile_keys = jax.random.split(jax.random.fold_in(key, 7), tile_total)
    chosen = jax.vmap(tile_choice)(tile_keys)
    return chosen.reshape(KRON_ROWS, KRON_COLS, MAXB).astype(jnp.int32)


def draw_sparse_rows(key, part):
    return (slot_positions(key) // (DS // BLK)).astype(jnp.int32)


def draw_sparse_cols(key, part):
    return (slot_positions(key) % (DS // BLK)).astype(jnp.int32)


def draw_sparse_count(key, part):
    tile_total = KRON_ROWS * KRON_COLS
    counts = jax.random.randint(jax.random.fold_in(key, 11), (tile_total,), 1, MAXB + 1)
    fullest = jax.random.randint(jax.random.fold_in(key, 13), (), 0, tile_total)
    counts = jnp.where(jnp.arange(tile_total) == fullest, MAXB, counts)
    return counts.reshape(KRON_ROWS, KRON_COLS).astype(jnp.int32)


def raised(entries, key, source, target, blocks, factor):
    owner, partner = [(jnp.arange(entries.shape[axis_at]) // (entries.shape[axis_at] // blocks)).reshape([-1 if axis == axis_at else 1 for axis in range(entries.ndim)]) for axis_at in (source, target)]
    chosen = jax.random.permutation(key, blocks)[partner]
    strong = (owner == chosen) | (owner == (partner + blocks // 2) % blocks)
    return jnp.where(strong, factor * entries, entries)


def level_of(rng, extent, cuts, low, top_value):
    gain = 1.0
    for axis_at, blocks in cuts:
        draws = jax.random.uniform(jax.random.fold_in(jax.random.fold_in(rng, 6), axis_at), (blocks,), jnp.float32, low / len(cuts), top_value / len(cuts))
        gain = gain * jnp.repeat(jnp.exp(draws), extent[axis_at] // blocks).reshape((-1,) + (1,) * (len(extent) - 1 - axis_at))
    return gain


def noise(rng, shape, width, most, cuts=(), held_as=jnp.bfloat16):
    factor_of = level_of(rng, shape, cuts, -0.22, 0.18) if cuts else 1.0
    drawn = jax.random.normal(rng, shape, jnp.float32) * width * factor_of
    return jnp.minimum(jnp.maximum(drawn, -most), most).astype(held_as)


def heavy_noise(stream_key, dims, scale, bound, pieces, heavy, kind=jnp.bfloat16):
    result = scale * jax.random.normal(stream_key, dims, jnp.float32)
    if pieces:
        result = result * level_of(stream_key, dims, pieces, -0.22, 0.18)
    return jnp.clip(raised(result, jax.random.fold_in(stream_key, 3), *heavy), -bound, bound).astype(kind)


def setup_inputs(seed: int = 0, part: int = 0) -> dict:
    splits = jax.random.split(jax.random.key(seed), 12)
    part_splits = jax.random.split(jax.random.fold_in(splits[11], part), 12)
    return {
        "hidden_in": heavy_noise(part_splits[0], (TOKENS, K), 1.0, 6.0, ((0, 4), (1, 4)), (1, 0, 4, 2.0)),
        "out_grad": heavy_noise(part_splits[1], (TOKENS, D), 1.0, 6.0, ((0, 4), (1, 4)), (1, 0, 4, 2.0)),
        "base_levels": draw_base_levels(jax.random.fold_in(splits[11], 71), part),
        "base_scales": jnp.clip(jnp.exp(math.log(0.015991211) - 0.6931472 * jax.random.uniform(splits[3], (K // QB, D), jnp.float32) ** level_of(splits[3], (K // QB, D), ((0, 4), (1, 4)), -0.2, 0.2)), 0.0079956055, 0.015991211).astype(jnp.bfloat16),
        "kron_outer": noise(splits[4], (KRON_ROWS, KRON_COLS), 0.6, 3.0, ((0, 4), (1, 4)), jnp.float32),
        "kron_left": noise(splits[5], (KT, R), KT ** -0.5, 0.078125),
        "kron_right": noise(splits[6], (R, DS), DS ** -0.5, 0.125),
        "sparse_rows": draw_sparse_rows(jax.random.fold_in(splits[11], 71), part),
        "sparse_cols": draw_sparse_cols(jax.random.fold_in(splits[11], 71), part),
        "sparse_count": draw_sparse_count(jax.random.fold_in(splits[11], 71), part),
        "sparse_values": noise(splits[10], (KRON_ROWS, KRON_COLS, MAXB, BLK, BLK), 0.02, 0.3125, ((0, 4), (1, 4))),
    }


def block_delta(rows_tile, cols_tile, count_tile, values_tile):
    slot_ids = jnp.arange(MAXB).astype(jnp.int32)
    live_slots = (slot_ids[None, :] < count_tile[:, None]).astype(jnp.float32)
    row_ids = jnp.arange(KT // BLK).astype(jnp.int32)
    col_ids = jnp.arange(DS // BLK).astype(jnp.int32)
    row_onehot = (rows_tile[..., None] == row_ids[None, None, :]).astype(jnp.float32) * live_slots[..., None]
    col_onehot = (cols_tile[..., None] == col_ids[None, None, :]).astype(jnp.float32)
    placed = jnp.einsum("sma,smb,smij->aisbj", row_onehot, col_onehot, values_tile.astype(jnp.float32), precision=lax.Precision.HIGHEST)
    return placed.reshape(KT, KRON_COLS * DS)


def reference(hidden_in, out_grad, base_levels, base_scales, kron_outer, kron_left, kron_right, sparse_rows, sparse_cols, sparse_count, sparse_values):
    highest = lax.Precision.HIGHEST
    grad_split = out_grad.reshape(TOKENS, KRON_COLS, DS)
    grad_proj = jnp.einsum("tsd,rd->str", grad_split.astype(jnp.float32), kron_right.astype(jnp.float32), precision=highest).astype(jnp.bfloat16)
    out_total = jnp.zeros((TOKENS, D), jnp.float32)
    left_grad = jnp.zeros((KT, R), jnp.float32)
    right_grad = jnp.zeros((R, DS), jnp.float32)
    grad_columns = []
    outer_rows = []
    sparse_tiles = []
    slot_ids = jnp.arange(MAXB).astype(jnp.int32)
    for tile_index in range(KRON_ROWS):
        first_row = tile_index * KT
        inputs_tile = hidden_in[:, first_row:first_row + KT]
        levels_tile = base_levels[first_row:first_row + KT].astype(jnp.float32)
        scales_tile = base_scales[first_row // QB:(first_row + KT) // QB].astype(jnp.float32)
        dequant = (levels_tile.reshape(KT // QB, QB, D) * scales_tile[:, None, :]).reshape(KT, D)
        sparse_delta = block_delta(sparse_rows[tile_index], sparse_cols[tile_index], sparse_count[tile_index], sparse_values[tile_index])
        weight = (dequant + sparse_delta).astype(jnp.bfloat16)
        projected = jnp.dot(inputs_tile, kron_left, preferred_element_type=jnp.float32).astype(jnp.bfloat16)
        low_rank = jnp.dot(projected, kron_right, preferred_element_type=jnp.float32)
        outer_row = kron_outer[tile_index]
        kron_part = (outer_row[None, :, None] * low_rank[:, None, :]).reshape(TOKENS, D)
        partial_value = jnp.dot(inputs_tile, weight, preferred_element_type=jnp.float32) + kron_part
        partial_value = lax.optimization_barrier(partial_value.astype(jnp.bfloat16))
        out_total = out_total + partial_value.astype(jnp.float32)
        mixed = jnp.einsum("s,str->tr", outer_row, grad_proj.astype(jnp.float32), precision=highest)
        back = lax.dot_general(out_grad, weight, (((1,), (1,)), ((), ())), preferred_element_type=jnp.float32)
        back = back + jnp.dot(mixed, kron_left.astype(jnp.float32).T, precision=highest)
        grad_columns.append(back.astype(jnp.bfloat16))
        outer_rows.append(jnp.einsum("tr,str->s", projected.astype(jnp.float32), grad_proj.astype(jnp.float32), precision=highest) / TOKENS)
        left_grad = left_grad + jnp.dot(inputs_tile.astype(jnp.float32).T, mixed, precision=highest) / TOKENS
        proj_out = lax.dot_general(projected, out_grad, (((0,), (0,)), ((), ())), preferred_element_type=jnp.float32).reshape(R, KRON_COLS, DS)
        right_grad = right_grad + jnp.einsum("s,rsd->rd", outer_row, proj_out, precision=highest) / TOKENS
        input_blocks = inputs_tile.reshape(TOKENS, KT // BLK, BLK)
        chosen_inputs = jnp.take(input_blocks, sparse_rows[tile_index], axis=1)
        grad_blocks = out_grad.reshape(TOKENS, KRON_COLS, DS // BLK, BLK)
        col_index = jnp.arange(KRON_COLS).astype(jnp.int32)[:, None]
        chosen_grads = grad_blocks[:, col_index, sparse_cols[tile_index], :]
        live_slots = (slot_ids[None, :] < sparse_count[tile_index][:, None]).astype(jnp.float32)
        blocks = jnp.einsum("tsmi,tsmj->smij", chosen_inputs.astype(jnp.float32), chosen_grads.astype(jnp.float32), precision=highest)
        sparse_tiles.append(blocks * live_slots[:, :, None, None] / TOKENS)
    layer_out = out_total.astype(jnp.bfloat16)
    input_grad = jnp.concatenate(grad_columns, axis=1)
    grad_outer = jnp.stack(outer_rows, axis=0)
    grad_sparse = jnp.stack(sparse_tiles, axis=0)
    return (layer_out, input_grad, grad_outer, left_grad, right_grad, grad_sparse)
```

```python
import functools

import jax
import jax.numpy as jnp
from jax import lax
from jax.experimental import pallas as pl
from jax.experimental.pallas import tpu as pltpu
from jax.sharding import PartitionSpec as P

F32 = jnp.float32
BF16 = jnp.bfloat16
MESH = pl.DeviceIdType.MESH
LANES = 128


def dot(a, b, ca, cb):
    return lax.dot_general(a, b, (((ca,), (cb,)), ((), ())), preferred_element_type=F32)


def splits(blocks, pieces):
    pieces = min(pieces, blocks)
    cuts = [blocks * i // pieces for i in range(pieces + 1)]
    return [(cuts[i] * LANES, (cuts[i + 1] - cuts[i]) * LANES) for i in range(pieces)]


def window(blocks, parts):
    width = -(-blocks // parts)
    return width, blocks - width, max(parts - 1, 1)


def kernel(
    shape,
    rows_ref, cols_ref, count_ref, coef_ref, x_hbm, dy_hbm, kl_hbm, kr_hbm, sc_hbm, val_hbm, w_hbm,
    out_parts, ig_parts, go_ref, gl_hbm, gr_hbm, gs_hbm,
    wv, xl, xs, dl, ds, klv, krv, scb, scf, vals, mapv, maps,
    igb, igr, igs, ob, proj_s, gproj_s, mx, ux, glq, glr, glp, gla, glw, glall, grq, grr, grp, gra, grw, grall, glo, gro, gso,
    w_sem, in_sem, map_sem, own_sem, xring_s, xring_r, xsub_s, xsub_r, dy_s, dy_r,
    igsub_s, igsub_r, ig_s, ig_r, ig_own, out_s, out_r, out_own, mx_s, mx_r, ux_s, ux_r,
    gl1_s, gl1_r, gl2_s, gl2_r, gl3_s, gl3_r, gr1_s, gr1_r, gr2_s, gr2_r, gr3_s, gr3_r, res_sem,
):
    n_t, n_d, n_c, own, kc, fc, pieces = shape
    n_s = n_d * n_c
    t, d, c = lax.axis_index("tp"), lax.axis_index("dp"), lax.axis_index("sub")
    s = d * n_c + c
    tile_rows, tile_cols = w_hbm.shape
    slots, block = val_hbm.shape[0], val_hbm.shape[1]
    col_blocks, row_blocks = tile_cols // block, tile_rows // block
    nb, nf = tile_rows // kc, tile_cols // fc
    pad = xs.shape[1] // n_s
    quant = tile_rows // sc_hbm.shape[0]
    inv = 1.0 / (own * n_s)
    coef = coef_ref[0, 0]

    def joined(ref, start, count):
        return jnp.concatenate([ref[start + i] for i in range(count)], axis=1)

    def all_x():
        return joined(xs, 0, row_blocks)

    def all_dy():
        return joined(ds, 0, col_blocks)

    def plane(h):
        o = lax.rem(s + h, n_s)
        return o, {"dp": o // n_c, "sub": lax.rem(o, n_c)}

    def along(h):
        o = lax.rem(t + h, n_t)
        return o, {"tp": o}

    def remote(src, dst, send, recv, where):
        return pltpu.make_async_remote_copy(
            src_ref=src, dst_ref=dst, send_sem=send, recv_sem=recv, device_id=where, device_id_type=MESH
        )

    barrier = pltpu.get_barrier_semaphore()
    for h in range(1, n_t):
        pl.semaphore_signal(barrier, inc=1, device_id=along(h)[1], device_id_type=MESH)
    for h in range(1, n_s):
        pl.semaphore_signal(barrier, inc=1, device_id=plane(h)[1], device_id_type=MESH)

    locals_ = [
        pltpu.make_async_copy(sc_hbm, scb, in_sem.at[0]),
        pltpu.make_async_copy(val_hbm, vals.at[pl.ds(0, slots)], in_sem.at[1]),
        pltpu.make_async_copy(kl_hbm, klv, in_sem.at[2]),
        pltpu.make_async_copy(kr_hbm, krv, in_sem.at[3]),
    ]
    own_x = pltpu.make_async_copy(x_hbm, xl.at[s], own_sem.at[0])
    own_dy = pltpu.make_async_copy(dy_hbm, dl.at[t], own_sem.at[1])

    def fetch(i):
        part = pl.ds(pl.multiple_of(i * kc, kc), kc)
        return pltpu.make_async_copy(w_hbm.at[part], wv.at[part], w_sem.at[i])

    for copy in locals_[:2]:
        copy.start()
    fetch(0).start()
    own_x.start()
    own_dy.start()
    for copy in locals_[2:]:
        copy.start()

    pl.semaphore_wait(barrier, n_t - 1 + n_s - 1)

    right, left = lax.rem(d + 1, n_d), lax.rem(d + n_d - 1, n_d)
    bounds = splits(row_blocks, pieces)

    def ring(h, p):
        q = lax.rem(d - h + 1 + n_d, n_d)
        cols = pl.ds(*bounds[p])
        src = x_hbm.at[:, cols] if h == 1 else xl.at[q * n_c + c, :, cols]
        return remote(src, xl.at[q * n_c + c, :, cols], xring_s.at[h - 1, p], xring_r.at[h - 1, p], {"dp": right})

    def ring_in(h, p):
        q = lax.rem(d - h + n_d, n_d)
        cols = pl.ds(*bounds[p])
        ref = xl.at[q * n_c + c, :, cols]
        return remote(ref, ref, xring_s.at[h - 1, p], xring_r.at[h - 1, p], {"dp": left})

    def across(h, p, core):
        q = lax.rem(d - h + n_d, n_d)
        cols = pl.ds(*bounds[p])
        ref = xl.at[q * n_c + core, :, cols]
        src = x_hbm.at[:, cols] if h == 0 else ref
        return remote(src, ref, xsub_s.at[h, p], xsub_r.at[h, p], {"sub": 1 - c})

    for h in range(1, n_t):
        o, where = along(h)
        remote(dy_hbm, dl.at[t], dy_s.at[h - 1], dy_r.at[h - 1], where).start()
    for p in range(len(bounds)):
        ring(1, p).start()
    for p in range(len(bounds)):
        across(0, p, c).start()

    @pl.loop(1, nb)
    def _(i):
        fetch(i).start()

    ids = lax.broadcasted_iota(jnp.int32, mapv.shape, 0) * LANES + lax.broadcasted_iota(jnp.int32, mapv.shape, 1)
    table = jnp.full(mapv.shape, slots, jnp.int32)
    for m in range(slots):
        key = jnp.where(m < count_ref[0, 0], rows_ref[0, 0, m] * col_blocks + cols_ref[0, 0, m], -1)
        table = jnp.where(ids == key, m, table)
    mapv[...] = table
    to_map = pltpu.make_async_copy(mapv, maps, map_sem.at[0])
    to_map.start()
    vals[slots] = jnp.zeros((block, block), BF16)
    tail = own // 8 * 8
    for o in range(n_s):
        xs[:, o * pad + tail:(o + 1) * pad, :] = jnp.zeros((row_blocks, pad - tail, block), BF16)
    for o in range(n_t):
        ds[:, o * pad + tail:(o + 1) * pad, :] = jnp.zeros((col_blocks, pad - tail, block), BF16)
    locals_[0].wait()
    locals_[1].wait()
    scf[...] = scb[...].astype(F32)
    to_map.wait()

    group = 4 if col_blocks % 4 == 0 else 1
    chunk_blocks = kc // block
    marks = [row_blocks * (40 + 15 * p) // 100 for p in range(len(bounds))]

    def pass_on(h, p):
        ring_in(h, p).wait_recv()
        if h < n_d - 1:
            ring(h + 1, p).start()
        across(h, p, c).start()

    @pl.loop(0, row_blocks)
    def _(rb):
        @pl.when(lax.rem(rb, chunk_blocks) == 0)
        def _():
            fetch(rb // chunk_blocks).wait()

        for p in range(len(bounds)):
            @pl.when(rb == marks[p])
            def _():
                pass_on(1, p)

        for cb in range(0, col_blocks, group):
            cut = slice(cb * block, (cb + group) * block)
            delta = []
            for i in range(group):
                b = rb * col_blocks + cb + i
                delta.append(vals[maps[b // LANES, lax.rem(b, LANES)]])
            delta = jnp.concatenate(delta, axis=1)
            for q in range(block // quant):
                part = pl.ds(pl.multiple_of(rb * block + q * quant, quant), quant)
                sc = scf[pl.ds(rb * (block // quant) + q, 1), cut]
                sc = jnp.broadcast_to(sc, (16, group * block)).astype(BF16)
                sc = jnp.broadcast_to(sc[None], (quant // 16, 16, group * block)).reshape(quant, group * block)
                wv[part, cut] = wv[part, cut] * sc + delta[q * quant:(q + 1) * quant]

    own_dy.wait()
    for h in range(1, n_t):
        o = lax.rem(t - h + n_t, n_t)
        remote(dl.at[o], dl.at[o], dy_s.at[h - 1], dy_r.at[h - 1], {"tp": o}).wait_recv()
    for o in range(n_t):
        for b in range(col_blocks):
            ds[b, o * pad:o * pad + own, :] = dl[o, :, b * block:(b + 1) * block]
    locals_[2].wait()
    locals_[3].wait()

    gproj = dot(krv[...], all_dy(), 1, 1).astype(BF16).astype(F32)
    gproj_s[...] = gproj.T.astype(BF16)
    mx[s] = coef * gproj
    for h in range(1, n_s):
        o, where = plane(h)
        remote(mx.at[s], mx.at[s], mx_s.at[h - 1], mx_r.at[h - 1], where).start()

    def back(j):
        part = pl.ds(pl.multiple_of(j * kc, kc), kc)
        b = dot(all_dy(), wv[part, :], 1, 1)
        b += coef * dot(gproj_s[...], klv[:, part], 1, 0)
        b = b.astype(BF16)
        for o in range(n_s):
            igb[j, o % n_c, (o // n_c) * pad:(o // n_c + 1) * pad, :] = b[o * pad:(o + 1) * pad]

    def igsub(j):
        return remote(igb.at[j, 1 - c], igr.at[j], igsub_s.at[j], igsub_r.at[j], {"sub": 1 - c})

    def ig_out(j, h):
        o = lax.rem(d + h, n_d)
        part = pl.ds(pl.multiple_of(j * kc, kc), kc)
        src = igs.at[j, pl.ds(pl.multiple_of(o * pad, pad), pad)]
        if h == 0:
            return pltpu.make_async_copy(src, ig_parts.at[d, :, part], ig_own.at[j])
        return remote(src, ig_parts.at[d, :, part], ig_s.at[h - 1, j], ig_r.at[h - 1, j], {"dp": o})

    def ig_in(j, h):
        o = lax.rem(d - h + n_d, n_d)
        part = pl.ds(pl.multiple_of(j * kc, kc), kc)
        ref = ig_parts.at[o, :, part]
        return remote(ref, ref, ig_s.at[h - 1, j], ig_r.at[h - 1, j], {"dp": o})

    def combine(j):
        igsub(j).wait_recv()
        igs[j] = (igb[j, c].astype(F32) + igr[j].astype(F32)).astype(BF16)
        for h in range(n_d):
            ig_out(j, h).start()

    def step_back(j):
        back(j)
        igsub(j).start()

        @pl.when(j > 0)
        def _():
            combine(j - 1)

    def ob_out(f, h):
        o = lax.rem(t + h, n_t)
        part = pl.ds(pl.multiple_of(f * fc, fc), fc)
        src = ob.at[f, pl.ds(pl.multiple_of(o * pad, pad), pad)]
        if h == 0:
            return pltpu.make_async_copy(src, out_parts.at[t, :, part], out_own.at[f])
        return remote(src, out_parts.at[t, :, part], out_s.at[h - 1, f], out_r.at[h - 1, f], {"tp": o})

    def ob_in(f, h):
        o = lax.rem(t - h + n_t, n_t)
        part = pl.ds(pl.multiple_of(f * fc, fc), fc)
        ref = out_parts.at[o, :, part]
        return remote(ref, ref, out_s.at[h - 1, f], out_r.at[h - 1, f], {"tp": o})

    def step_forward(f):
        part = pl.ds(pl.multiple_of(f * fc, fc), fc)
        o = dot(all_x(), wv[:, part], 1, 0)
        o += coef * dot(proj_s[...], krv[:, part], 1, 0)
        ob[f] = o.astype(BF16)
        for h in range(n_t):
            ob_out(f, h).start()

    ks, ks_free, ks_den = window(row_blocks, n_s)
    kt, kt_free, kt_den = window(ks, n_t)
    rt, rt_free, rt_den = window(col_blocks, n_t)
    rs, rs_free, rs_den = window(rt, n_s)

    def cut_of(i, width, free, den):
        return pl.ds(pl.multiple_of((i * free // den) * LANES, LANES), width * LANES)

    def exchange(n, hop, src, dst, me, send, recv):
        out = []
        for h in range(1, n):
            o, where = hop(h)
            out.append(remote(src(o), dst.at[me], send.at[h - 1], recv.at[h - 1], where))
        return out

    def arrivals(n, hop, dst, send, recv):
        for h in range(1, n):
            o, where = hop(n - h)
            remote(dst.at[o], dst.at[o], send.at[h - 1], recv.at[h - 1], where).wait_recv()

    ex_mx = lambda: exchange(n_s, plane, lambda o: mx.at[s], mx, s, mx_s, mx_r)
    ex_ux = lambda: exchange(n_t, along, lambda o: ux.at[t], ux, t, ux_s, ux_r)
    ex_gl1 = lambda: exchange(n_t, along, lambda o: glq.at[:, cut_of(o, kt, kt_free, kt_den)], glr, t, gl1_s, gl1_r)
    ex_gr1 = lambda: exchange(n_s, plane, lambda o: grq.at[:, cut_of(o, rs, rs_free, rs_den)], grr, s, gr1_s, gr1_r)
    ex_gl2 = lambda: exchange(n_t, along, lambda o: glp, gla, t, gl2_s, gl2_r)
    ex_gr2 = lambda: exchange(n_s, plane, lambda o: grp, gra, s, gr2_s, gr2_r)
    ex_gl3 = lambda: exchange(n_s, plane, lambda o: glw, glall, s, gl3_s, gl3_r)
    ex_gr3 = lambda: exchange(n_t, along, lambda o: grw, grall, t, gr3_s, gr3_r)

    def stage0():
        arrivals(n_s, plane, mx, mx_s, mx_r)
        arrivals(n_t, along, ux, ux_s, ux_r)
        mixed = mx[0]
        for o in range(1, n_s):
            mixed += mx[o]
        used = ux[0]
        for o in range(1, n_t):
            used += ux[o]
        g = dot(mixed.astype(BF16), joined(xs, s * ks_free // ks_den, ks), 1, 0) * inv
        glq[...] = g.astype(BF16)
        glr[t] = glq[:, cut_of(t, kt, kt_free, kt_den)]
        grq[...] = dot(used.astype(BF16), joined(ds, t * rt_free // rt_den, rt), 1, 0) * inv
        grr[s] = grq[:, cut_of(s, rs, rs_free, rs_den)]
        for copy in ex_gl1() + ex_gr1():
            copy.start()

    def stage1():
        arrivals(n_t, along, glr, gl1_s, gl1_r)
        arrivals(n_s, plane, grr, gr1_s, gr1_r)
        g = glr[0].astype(F32)
        for o in range(1, n_t):
            g += glr[o].astype(F32)
        glp[...] = g.astype(BF16)
        gla[t] = g.astype(BF16)
        g = grr[0]
        for o in range(1, n_s):
            g += grr[o]
        grp[...] = g
        gra[s] = g
        for copy in ex_gl2() + ex_gr2():
            copy.start()

    def stage2():
        arrivals(n_t, along, gla, gl2_s, gl2_r)
        arrivals(n_s, plane, gra, gr2_s, gr2_r)
        for o in range(n_t):
            a = (o * kt_free // kt_den) * LANES
            glw[:, a:a + kt * LANES] = gla[o]
            glall[s, :, a:a + kt * LANES] = gla[o]
        for o in range(n_s):
            a = (o * rs_free // rs_den) * LANES
            grw[:, a:a + rs * LANES] = gra[o]
            grall[t, :, a:a + rs * LANES] = gra[o]
        for copy in ex_gl3() + ex_gr3():
            copy.start()

    gl_out = pltpu.make_async_copy(glo, gl_hbm, res_sem.at[0])
    gr_out = pltpu.make_async_copy(gro, gr_hbm, res_sem.at[1])
    gs_out = pltpu.make_async_copy(gso, gs_hbm, res_sem.at[2])

    def stage3():
        arrivals(n_s, plane, glall, gl3_s, gl3_r)
        arrivals(n_t, along, grall, gr3_s, gr3_r)
        for o in range(n_s):
            a = (o * ks_free // ks_den) * LANES
            glo[:, a:a + ks * LANES] = glall[o].astype(F32)
        for o in range(n_t):
            a = (o * rt_free // rt_den) * LANES
            gro[:, a:a + rt * LANES] = grall[o]
        gl_out.start()
        gr_out.start()

    per = (nb - 1) // nf
    first = nb - per * nf

    @pl.loop(0, first)
    def _(j):
        step_back(j)

    for h in range(2, n_d):
        for p in range(len(bounds)):
            pass_on(h, p)
    own_x.wait()
    for h in range(n_d):
        for p in range(len(bounds)):
            across(h, p, 1 - c).wait_recv()
    for o in range(n_s):
        for b in range(row_blocks):
            xs[b, o * pad:o * pad + own, :] = xl[o, :, b * block:(b + 1) * block]

    proj = dot(klv[...], all_x(), 1, 1).astype(BF16).astype(F32)
    proj_s[...] = proj.T.astype(BF16)
    ux[t] = coef * proj
    for copy in ex_ux():
        copy.start()
    go_ref[...] = (jnp.sum(proj * gproj) * inv).reshape(1, 1)

    @pl.loop(0, slots)
    def _(m):
        xr = xs[rows_ref[0, 0, m]]
        dc = ds[cols_ref[0, 0, m]]
        live = jnp.where(m < count_ref[0, 0], inv, 0.0)
        gso[m] = dot(xr, dc, 0, 0) * live

    gs_out.start()

    stages = [stage0, stage1, stage2]

    @pl.loop(0, nf)
    def _(f):
        @pl.loop(0, per)
        def _(i):
            step_back(first + f * per + i)

        for k in range(min(nf, len(stages))):
            @pl.when(f == k)
            def _():
                stages[k]()

        step_forward(f)

    combine(nb - 1)
    for k in range(nf, len(stages)):
        stages[k]()
    stage3()

    for copy in ex_mx() + ex_ux() + ex_gl1() + ex_gr1() + ex_gl2() + ex_gr2() + ex_gl3() + ex_gr3():
        copy.wait_send()
    for h in range(1, n_t):
        remote(dy_hbm, dl.at[t], dy_s.at[h - 1], dy_r.at[h - 1], along(h)[1]).wait_send()
    for p in range(len(bounds)):
        for h in range(1, n_d):
            ring(h, p).wait_send()
        for h in range(n_d):
            across(h, p, c).wait_send()

    @pl.loop(0, nb)
    def _(j):
        igsub(j).wait_send()
        ig_out(j, 0).wait()
        for h in range(1, n_d):
            ig_out(j, h).wait_send()
            ig_in(j, h).wait_recv()

    @pl.loop(0, nf)
    def _(f):
        ob_out(f, 0).wait()
        for h in range(1, n_t):
            ob_out(f, h).wait_send()
            ob_in(f, h).wait_recv()

    gl_out.wait()
    gr_out.wait()
    gs_out.wait()


def shards(
    hidden_in, out_grad, base_levels, base_scales, kron_outer, kron_left, kron_right,
    sparse_rows, sparse_cols, sparse_count, sparse_values,
):
    tile_rows, tile_cols = base_levels.shape
    slots, block = sparse_values.shape[2], sparse_values.shape[3]
    own = hidden_in.shape[0]
    pad = own + -own % 16
    rank = kron_left.shape[1]
    row_blocks, col_blocks = tile_rows // block, tile_cols // block
    n_d, n_c, n_t = lax.axis_size("dp"), lax.axis_size("sub"), lax.axis_size("tp")
    n_s = n_d * n_c
    full = n_s * pad
    kc = 4 * block if row_blocks % 4 == 0 else block
    fc = 4 * block if col_blocks % 4 == 0 else block
    nb, nf = tile_rows // kc, tile_cols // fc
    pieces = min(4, row_blocks)
    ks = window(row_blocks, n_s)[0]
    kt = window(ks, n_t)[0]
    rt = window(col_blocks, n_t)[0]
    rs = window(rt, n_s)[0]
    table_rows = -(-(row_blocks * col_blocks) // (8 * LANES)) * 8
    vmem = pl.BlockSpec(memory_space=pltpu.VMEM)
    smem = pl.BlockSpec(memory_space=pltpu.SMEM)
    any_ = pl.BlockSpec(memory_space=pl.ANY)
    dma = pltpu.SemaphoreType.DMA
    out_parts, ig_parts, go, gl, gr, gs = pl.pallas_call(
        functools.partial(kernel, (n_t, n_d, n_c, own, kc, fc, pieces)),
        in_specs=[smem] * 4 + [any_] * 7,
        out_specs=[any_, any_, vmem, any_, any_, any_],
        out_shape=[
            jax.ShapeDtypeStruct((n_t, pad, tile_cols), BF16),
            jax.ShapeDtypeStruct((n_d, pad, tile_rows), BF16),
            jax.ShapeDtypeStruct((1, 1), F32),
            jax.ShapeDtypeStruct((rank, tile_rows), F32),
            jax.ShapeDtypeStruct((rank, tile_cols), F32),
            jax.ShapeDtypeStruct((slots, block, block), F32),
        ],
        scratch_shapes=[
            pltpu.VMEM((tile_rows, tile_cols), BF16),
            pltpu.VMEM((n_s, own, tile_rows), BF16),
            pltpu.VMEM((row_blocks, full, block), BF16),
            pltpu.VMEM((n_t, own, tile_cols), BF16),
            pltpu.VMEM((col_blocks, full, block), BF16),
            pltpu.VMEM((rank, tile_rows), BF16),
            pltpu.VMEM((rank, tile_cols), BF16),
            pltpu.VMEM(base_scales.shape, BF16),
            pltpu.VMEM(base_scales.shape, F32),
            pltpu.VMEM((slots + 1, block, block), BF16),
            pltpu.VMEM((table_rows, LANES), jnp.int32),
            pltpu.SMEM((table_rows, LANES), jnp.int32),
            pltpu.VMEM((nb, n_c, n_d * pad, kc), BF16),
            pltpu.VMEM((nb, n_d * pad, kc), BF16),
            pltpu.VMEM((nb, n_d * pad, kc), BF16),
            pltpu.VMEM((nf, full, fc), BF16),
            pltpu.VMEM((full, rank), BF16),
            pltpu.VMEM((full, rank), BF16),
            pltpu.VMEM((n_s, rank, full), F32),
            pltpu.VMEM((n_t, rank, full), F32),
            pltpu.VMEM((rank, ks * LANES), BF16),
            pltpu.VMEM((n_t, rank, kt * LANES), BF16),
            pltpu.VMEM((rank, kt * LANES), BF16),
            pltpu.VMEM((n_t, rank, kt * LANES), BF16),
            pltpu.VMEM((rank, ks * LANES), BF16),
            pltpu.VMEM((n_s, rank, ks * LANES), BF16),
            pltpu.VMEM((rank, rt * LANES), F32),
            pltpu.VMEM((n_s, rank, rs * LANES), F32),
            pltpu.VMEM((rank, rs * LANES), F32),
            pltpu.VMEM((n_s, rank, rs * LANES), F32),
            pltpu.VMEM((rank, rt * LANES), F32),
            pltpu.VMEM((n_t, rank, rt * LANES), F32),
            pltpu.VMEM((rank, tile_rows), F32),
            pltpu.VMEM((rank, tile_cols), F32),
            pltpu.VMEM((slots, block, block), F32),
            dma((nb,)), dma((4,)), dma((1,)), dma((2,)),
            dma((n_d - 1, pieces)), dma((n_d - 1, pieces)), dma((n_d, pieces)), dma((n_d, pieces)),
            dma((n_t - 1,)), dma((n_t - 1,)),
            dma((nb,)), dma((nb,)), dma((n_d - 1, nb)), dma((n_d - 1, nb)), dma((nb,)),
            dma((n_t - 1, nf)), dma((n_t - 1, nf)), dma((nf,)),
            dma((n_s - 1,)), dma((n_s - 1,)), dma((n_t - 1,)), dma((n_t - 1,)),
            dma((n_t - 1,)), dma((n_t - 1,)), dma((n_t - 1,)), dma((n_t - 1,)), dma((n_s - 1,)), dma((n_s - 1,)),
            dma((n_s - 1,)), dma((n_s - 1,)), dma((n_s - 1,)), dma((n_s - 1,)), dma((n_t - 1,)), dma((n_t - 1,)),
            dma((3,)),
        ],
        compiler_params=pltpu.CompilerParams(
            vmem_limit_bytes=60 << 20, collective_id=0, has_side_effects=True
        ),
    )(
        sparse_rows, sparse_cols, sparse_count, kron_outer, hidden_in, out_grad, kron_left.T, kron_right,
        base_scales, sparse_values[0, 0], base_levels,
    )
    layer_out = jnp.sum(out_parts.astype(F32), axis=0).astype(BF16)[:own]
    input_grad = jnp.sum(ig_parts.astype(F32), axis=0).astype(BF16)[:own]
    return layer_out, input_grad, go, gl.T, gr, gs[None, None]


def solution(mesh):
    return jax.shard_map(
        shards,
        mesh=mesh,
        in_specs=(
            P(("grp", "dp", "sub"), "tp"),
            P(("grp", "tp"), ("dp", "sub")),
            P("tp", ("dp", "sub")),
            P("tp", ("dp", "sub")),
            P("tp", ("dp", "sub")),
            P(),
            P(),
            P("tp", ("dp", "sub"), None),
            P("tp", ("dp", "sub"), None),
            P("tp", ("dp", "sub")),
            P("tp", ("dp", "sub"), None, None, None),
        ),
        out_specs=(
            P(("grp", "tp"), ("dp", "sub")),
            P(("grp", "dp", "sub"), "tp"),
            P(("grp", "tp"), ("dp", "sub")),
            P("grp", None),
            P("grp", None),
            P(("grp", "tp"), ("dp", "sub"), None, None, None),
        ),
        check_vma=False,
    )
```

```python
import functools

import jax
import jax.numpy as jnp
from jax import lax
from jax.experimental import pallas as pl
from jax.experimental.pallas import tpu as pltpu
from jax.sharding import PartitionSpec as P

F32 = jnp.float32
BF16 = jnp.bfloat16
MESH = pl.DeviceIdType.MESH
LANES = 128


def dot(a, b, ca, cb):
    return lax.dot_general(a, b, (((ca,), (cb,)), ((), ())), preferred_element_type=F32)


def splits(blocks, pieces):
    pieces = min(pieces, blocks)
    cuts = [blocks * i // pieces for i in range(pieces + 1)]
    return [(cuts[i] * LANES, (cuts[i + 1] - cuts[i]) * LANES) for i in range(pieces)]


def window(blocks, parts):
    width = -(-blocks // parts)
    return width, blocks - width, max(parts - 1, 1)


def kernel(
    shape,
    rows_ref, cols_ref, count_ref, coef_ref, x_hbm, dy_hbm, kl_hbm, kr_hbm, sc_hbm, val_hbm, w_hbm,
    out_parts, ig_parts, go_ref, gl_hbm, gr_hbm, gs_hbm,
    wv, xl, xs, dl, ds, klv, krv, scb, scf, vals, mapv, maps,
    igb, igr, igs, ob, proj_s, gproj_s, mx, ux, glq, glr, glp, gla, glw, glall, grq, grr, grp, gra, grw, grall, glo, gro, gso,
    w_sem, in_sem, map_sem, own_sem, xring_s, xring_r, xsub_s, xsub_r, dy_s, dy_r,
    igsub_s, igsub_r, ig_s, ig_r, ig_own, out_s, out_r, out_own, mx_s, mx_r, ux_s, ux_r,
    gl1_s, gl1_r, gl2_s, gl2_r, gl3_s, gl3_r, gr1_s, gr1_r, gr2_s, gr2_r, gr3_s, gr3_r, res_sem,
):
    n_t, n_d, n_c, own, kc, fc, pieces = shape
    n_s = n_d * n_c
    t, d, c = lax.axis_index("tp"), lax.axis_index("dp"), lax.axis_index("sub")
    s = d * n_c + c
    tile_rows, tile_cols = w_hbm.shape
    slots, block = val_hbm.shape[0], val_hbm.shape[1]
    col_blocks, row_blocks = tile_cols // block, tile_rows // block
    nb, nf = tile_rows // kc, tile_cols // fc
    pad = xs.shape[1] // n_s
    quant = tile_rows // sc_hbm.shape[0]
    inv = 1.0 / (own * n_s)
    coef = coef_ref[0, 0]

    def joined(ref, start, count):
        return jnp.concatenate([ref[start + i] for i in range(count)], axis=1)

    def all_x():
        return joined(xs, 0, row_blocks)

    def all_dy():
        return joined(ds, 0, col_blocks)

    def plane(h):
        o = lax.rem(s + h, n_s)
        return o, {"dp": o // n_c, "sub": lax.rem(o, n_c)}

    def along(h):
        o = lax.rem(t + h, n_t)
        return o, {"tp": o}

    def remote(src, dst, send, recv, where):
        return pltpu.make_async_remote_copy(
            src_ref=src, dst_ref=dst, send_sem=send, recv_sem=recv, device_id=where, device_id_type=MESH
        )

    barrier = pltpu.get_barrier_semaphore()
    for h in range(1, n_t):
        pl.semaphore_signal(barrier, inc=1, device_id=along(h)[1], device_id_type=MESH)
    for h in range(1, n_s):
        pl.semaphore_signal(barrier, inc=1, device_id=plane(h)[1], device_id_type=MESH)

    locals_ = [
        pltpu.make_async_copy(sc_hbm, scb, in_sem.at[0]),
        pltpu.make_async_copy(val_hbm, vals.at[pl.ds(0, slots)], in_sem.at[1]),
        pltpu.make_async_copy(kl_hbm, klv, in_sem.at[2]),
        pltpu.make_async_copy(kr_hbm, krv, in_sem.at[3]),
    ]
    own_x = pltpu.make_async_copy(x_hbm, xl.at[s], own_sem.at[0])
    own_dy = pltpu.make_async_copy(dy_hbm, dl.at[t], own_sem.at[1])

    def fetch(i):
        part = pl.ds(pl.multiple_of(i * kc, kc), kc)
        return pltpu.make_async_copy(w_hbm.at[part], wv.at[part], w_sem.at[i])

    for copy in locals_[:2]:
        copy.start()
    own_x.start()
    own_dy.start()
    for copy in locals_[2:]:
        copy.start()

    @pl.loop(0, nb)
    def _(i):
        fetch(i).start()

    pl.semaphore_wait(barrier, n_t - 1 + n_s - 1)

    right, left = lax.rem(d + 1, n_d), lax.rem(d + n_d - 1, n_d)
    bounds = splits(row_blocks, pieces)

    def ring(h, p):
        q = lax.rem(d - h + 1 + n_d, n_d)
        cols = pl.ds(*bounds[p])
        src = x_hbm.at[:, cols] if h == 1 else xl.at[q * n_c + c, :, cols]
        return remote(src, xl.at[q * n_c + c, :, cols], xring_s.at[h - 1, p], xring_r.at[h - 1, p], {"dp": right})

    def ring_in(h, p):
        q = lax.rem(d - h + n_d, n_d)
        cols = pl.ds(*bounds[p])
        ref = xl.at[q * n_c + c, :, cols]
        return remote(ref, ref, xring_s.at[h - 1, p], xring_r.at[h - 1, p], {"dp": left})

    def across(h, p, core):
        q = lax.rem(d - h + n_d, n_d)
        cols = pl.ds(*bounds[p])
        ref = xl.at[q * n_c + core, :, cols]
        src = x_hbm.at[:, cols] if h == 0 else ref
        return remote(src, ref, xsub_s.at[h, p], xsub_r.at[h, p], {"sub": 1 - c})

    for h in range(1, n_t):
        o, where = along(h)
        remote(dy_hbm, dl.at[t], dy_s.at[h - 1], dy_r.at[h - 1], where).start()
    for p in range(len(bounds)):
        ring(1, p).start()
    for p in range(len(bounds)):
        across(0, p, c).start()

    ids = lax.broadcasted_iota(jnp.int32, mapv.shape, 0) * LANES + lax.broadcasted_iota(jnp.int32, mapv.shape, 1)
    table = jnp.full(mapv.shape, slots, jnp.int32)
    for m in range(slots):
        key = jnp.where(m < count_ref[0, 0], rows_ref[0, 0, m] * col_blocks + cols_ref[0, 0, m], -1)
        table = jnp.where(ids == key, m, table)
    mapv[...] = table
    to_map = pltpu.make_async_copy(mapv, maps, map_sem.at[0])
    to_map.start()
    vals[slots] = jnp.zeros((block, block), BF16)
    tail = own // 8 * 8
    for o in range(n_s):
        xs[:, o * pad + tail:(o + 1) * pad, :] = jnp.zeros((row_blocks, pad - tail, block), BF16)
    for o in range(n_t):
        ds[:, o * pad + tail:(o + 1) * pad, :] = jnp.zeros((col_blocks, pad - tail, block), BF16)
    locals_[0].wait()
    locals_[1].wait()
    scf[...] = scb[...].astype(F32)
    to_map.wait()

    group = 4 if col_blocks % 4 == 0 else 1
    chunk_blocks = kc // block
    marks = [row_blocks * (40 + 15 * p) // 100 for p in range(len(bounds))]

    def pass_on(h, p):
        ring_in(h, p).wait_recv()
        if h < n_d - 1:
            ring(h + 1, p).start()
        across(h, p, c).start()

    @pl.loop(0, row_blocks)
    def _(rb):
        @pl.when(lax.rem(rb, chunk_blocks) == 0)
        def _():
            fetch(rb // chunk_blocks).wait()

        for p in range(len(bounds)):
            @pl.when(rb == marks[p])
            def _():
                pass_on(1, p)

        for cb in range(0, col_blocks, group):
            cut = slice(cb * block, (cb + group) * block)
            delta = []
            for i in range(group):
                b = rb * col_blocks + cb + i
                delta.append(vals[maps[b // LANES, lax.rem(b, LANES)]])
            delta = jnp.concatenate(delta, axis=1)
            for q in range(block // quant):
                part = pl.ds(pl.multiple_of(rb * block + q * quant, quant), quant)
                sc = scf[pl.ds(rb * (block // quant) + q, 1), cut]
                sc = jnp.broadcast_to(sc, (16, group * block)).astype(BF16)
                sc = jnp.broadcast_to(sc[None], (quant // 16, 16, group * block)).reshape(quant, group * block)
                wv[part, cut] = wv[part, cut] * sc + delta[q * quant:(q + 1) * quant]

    def back(j):
        part = pl.ds(pl.multiple_of(j * kc, kc), kc)
        b = dot(all_dy(), wv[part, :], 1, 1)
        b += coef * dot(gproj_s[...], klv[:, part], 1, 0)
        b = b.astype(BF16)
        for o in range(n_s):
            igb[j, o % n_c, (o // n_c) * pad:(o // n_c + 1) * pad, :] = b[o * pad:(o + 1) * pad]

    def igsub(j):
        return remote(igb.at[j, 1 - c], igr.at[j], igsub_s.at[j], igsub_r.at[j], {"sub": 1 - c})

    def ig_out(j, h):
        o = lax.rem(d + h, n_d)
        part = pl.ds(pl.multiple_of(j * kc, kc), kc)
        src = igs.at[j, pl.ds(pl.multiple_of(o * pad, pad), pad)]
        if h == 0:
            return pltpu.make_async_copy(src, ig_parts.at[d, :, part], ig_own.at[j])
        return remote(src, ig_parts.at[d, :, part], ig_s.at[h - 1, j], ig_r.at[h - 1, j], {"dp": o})

    def ig_in(j, h):
        o = lax.rem(d - h + n_d, n_d)
        part = pl.ds(pl.multiple_of(j * kc, kc), kc)
        ref = ig_parts.at[o, :, part]
        return remote(ref, ref, ig_s.at[h - 1, j], ig_r.at[h - 1, j], {"dp": o})

    def combine(j):
        igsub(j).wait_recv()
        igs[j] = (igb[j, c].astype(F32) + igr[j].astype(F32)).astype(BF16)
        for h in range(n_d):
            ig_out(j, h).start()

    def step_back(j):
        back(j)
        igsub(j).start()

        @pl.when(j > 0)
        def _():
            combine(j - 1)

    def ob_out(f, h):
        o = lax.rem(t + h, n_t)
        part = pl.ds(pl.multiple_of(f * fc, fc), fc)
        src = ob.at[f, pl.ds(pl.multiple_of(o * pad, pad), pad)]
        if h == 0:
            return pltpu.make_async_copy(src, out_parts.at[t, :, part], out_own.at[f])
        return remote(src, out_parts.at[t, :, part], out_s.at[h - 1, f], out_r.at[h - 1, f], {"tp": o})

    def ob_in(f, h):
        o = lax.rem(t - h + n_t, n_t)
        part = pl.ds(pl.multiple_of(f * fc, fc), fc)
        ref = out_parts.at[o, :, part]
        return remote(ref, ref, out_s.at[h - 1, f], out_r.at[h - 1, f], {"tp": o})

    def step_forward(f):
        part = pl.ds(pl.multiple_of(f * fc, fc), fc)
        o = dot(all_x(), wv[:, part], 1, 0)
        o += coef * dot(proj_s[...], krv[:, part], 1, 0)
        ob[f] = o.astype(BF16)
        for h in range(n_t):
            ob_out(f, h).start()

    ks, ks_free, ks_den = window(row_blocks, n_s)
    kt, kt_free, kt_den = window(ks, n_t)
    rt, rt_free, rt_den = window(col_blocks, n_t)
    rs, rs_free, rs_den = window(rt, n_s)

    def cut_of(i, width, free, den):
        return pl.ds(pl.multiple_of((i * free // den) * LANES, LANES), width * LANES)

    def exchange(n, hop, src, dst, me, send, recv):
        out = []
        for h in range(1, n):
            o, where = hop(h)
            out.append(remote(src(o), dst.at[me], send.at[h - 1], recv.at[h - 1], where))
        return out

    def arrivals(n, hop, dst, send, recv):
        for h in range(1, n):
            o, where = hop(n - h)
            remote(dst.at[o], dst.at[o], send.at[h - 1], recv.at[h - 1], where).wait_recv()

    ex_mx = lambda: exchange(n_s, plane, lambda o: mx.at[s], mx, s, mx_s, mx_r)
    ex_ux = lambda: exchange(n_t, along, lambda o: ux.at[t], ux, t, ux_s, ux_r)
    ex_gl1 = lambda: exchange(n_t, along, lambda o: glq.at[:, cut_of(o, kt, kt_free, kt_den)], glr, t, gl1_s, gl1_r)
    ex_gr1 = lambda: exchange(n_s, plane, lambda o: grq.at[:, cut_of(o, rs, rs_free, rs_den)], grr, s, gr1_s, gr1_r)
    ex_gl2 = lambda: exchange(n_t, along, lambda o: glp, gla, t, gl2_s, gl2_r)
    ex_gr2 = lambda: exchange(n_s, plane, lambda o: grp, gra, s, gr2_s, gr2_r)
    ex_gl3 = lambda: exchange(n_s, plane, lambda o: glw, glall, s, gl3_s, gl3_r)
    ex_gr3 = lambda: exchange(n_t, along, lambda o: grw, grall, t, gr3_s, gr3_r)

    def stage0():
        arrivals(n_s, plane, mx, mx_s, mx_r)
        arrivals(n_t, along, ux, ux_s, ux_r)
        mixed = mx[0]
        for o in range(1, n_s):
            mixed += mx[o]
        used = ux[0]
        for o in range(1, n_t):
            used += ux[o]
        g = dot(mixed.astype(BF16), joined(xs, s * ks_free // ks_den, ks), 1, 0) * inv
        glq[...] = g.astype(BF16)
        glr[t] = glq[:, cut_of(t, kt, kt_free, kt_den)]
        grq[...] = dot(used.astype(BF16), joined(ds, t * rt_free // rt_den, rt), 1, 0) * inv
        grr[s] = grq[:, cut_of(s, rs, rs_free, rs_den)]
        for copy in ex_gl1() + ex_gr1():
            copy.start()

    def stage1():
        arrivals(n_t, along, glr, gl1_s, gl1_r)
        arrivals(n_s, plane, grr, gr1_s, gr1_r)
        g = glr[0].astype(F32)
        for o in range(1, n_t):
            g += glr[o].astype(F32)
        glp[...] = g.astype(BF16)
        gla[t] = g.astype(BF16)
        g = grr[0]
        for o in range(1, n_s):
            g += grr[o]
        grp[...] = g
        gra[s] = g
        for copy in ex_gl2() + ex_gr2():
            copy.start()

    def stage2():
        arrivals(n_t, along, gla, gl2_s, gl2_r)
        arrivals(n_s, plane, gra, gr2_s, gr2_r)
        for o in range(n_t):
            a = (o * kt_free // kt_den) * LANES
            glw[:, a:a + kt * LANES] = gla[o]
            glall[s, :, a:a + kt * LANES] = gla[o]
        for o in range(n_s):
            a = (o * rs_free // rs_den) * LANES
            grw[:, a:a + rs * LANES] = gra[o]
            grall[t, :, a:a + rs * LANES] = gra[o]
        for copy in ex_gl3() + ex_gr3():
            copy.start()

    gl_out = pltpu.make_async_copy(glo, gl_hbm, res_sem.at[0])
    gr_out = pltpu.make_async_copy(gro, gr_hbm, res_sem.at[1])
    gs_out = pltpu.make_async_copy(gso, gs_hbm, res_sem.at[2])

    def stage3():
        arrivals(n_s, plane, glall, gl3_s, gl3_r)
        arrivals(n_t, along, grall, gr3_s, gr3_r)
        for o in range(n_s):
            a = (o * ks_free // ks_den) * LANES
            glo[:, a:a + ks * LANES] = glall[o].astype(F32)
        for o in range(n_t):
            a = (o * rt_free // rt_den) * LANES
            gro[:, a:a + rt * LANES] = grall[o]
        gl_out.start()
        gr_out.start()

    for h in range(2, n_d):
        for p in range(len(bounds)):
            pass_on(h, p)
    own_dy.wait()
    for h in range(1, n_t):
        o = lax.rem(t - h + n_t, n_t)
        remote(dl.at[o], dl.at[o], dy_s.at[h - 1], dy_r.at[h - 1], {"tp": o}).wait_recv()
    for o in range(n_t):
        for b in range(col_blocks):
            ds[b, o * pad:o * pad + own, :] = dl[o, :, b * block:(b + 1) * block]
    locals_[2].wait()
    locals_[3].wait()

    gproj = dot(krv[...], all_dy(), 1, 1).astype(BF16).astype(F32)
    gproj_s[...] = gproj.T.astype(BF16)
    mx[s] = coef * gproj
    for h in range(1, n_s):
        o, where = plane(h)
        remote(mx.at[s], mx.at[s], mx_s.at[h - 1], mx_r.at[h - 1], where).start()

    own_x.wait()
    for h in range(n_d):
        for p in range(len(bounds)):
            across(h, p, 1 - c).wait_recv()
    for o in range(n_s):
        for b in range(row_blocks):
            xs[b, o * pad:o * pad + own, :] = xl[o, :, b * block:(b + 1) * block]

    proj = dot(klv[...], all_x(), 1, 1).astype(BF16).astype(F32)
    proj_s[...] = proj.T.astype(BF16)
    ux[t] = coef * proj
    for copy in ex_ux():
        copy.start()
    go_ref[...] = (jnp.sum(proj * gproj) * inv).reshape(1, 1)

    per = nb // nf
    stages = [stage0, stage1, stage2]

    @pl.loop(0, nf)
    def _(f):
        for k in range(min(nf - 1, len(stages))):
            @pl.when(f == k + 1)
            def _():
                stages[k]()

        step_forward(f)

        @pl.loop(0, per)
        def _(i):
            step_back(f * per + i)

    @pl.loop(nf * per, nb)
    def _(j):
        step_back(j)

    combine(nb - 1)
    for k in range(nf - 1, len(stages)):
        stages[k]()

    @pl.loop(0, slots)
    def _(m):
        xr = xs[rows_ref[0, 0, m]]
        dc = ds[cols_ref[0, 0, m]]
        live = jnp.where(m < count_ref[0, 0], inv, 0.0)
        gso[m] = dot(xr, dc, 0, 0) * live

    gs_out.start()
    stage3()

    for copy in ex_mx() + ex_ux() + ex_gl1() + ex_gr1() + ex_gl2() + ex_gr2() + ex_gl3() + ex_gr3():
        copy.wait_send()
    for h in range(1, n_t):
        remote(dy_hbm, dl.at[t], dy_s.at[h - 1], dy_r.at[h - 1], along(h)[1]).wait_send()
    for p in range(len(bounds)):
        for h in range(1, n_d):
            ring(h, p).wait_send()
        for h in range(n_d):
            across(h, p, c).wait_send()

    @pl.loop(0, nb)
    def _(j):
        igsub(j).wait_send()
        ig_out(j, 0).wait()
        for h in range(1, n_d):
            ig_out(j, h).wait_send()
            ig_in(j, h).wait_recv()

    @pl.loop(0, nf)
    def _(f):
        ob_out(f, 0).wait()
        for h in range(1, n_t):
            ob_out(f, h).wait_send()
            ob_in(f, h).wait_recv()

    gl_out.wait()
    gr_out.wait()
    gs_out.wait()


def finish(
    out_parts, ig_parts, go_in, gl_in, gr_in, gs_in, out_hbm, ig_hbm, go_ref, gl_hbm, gr_hbm, gs_hbm,
    op, ip, glv, grv, gsv, ov, iv, in_sem, out_sem,
):
    own = ov.shape[0]
    passed = [(gs_in, gsv, gs_hbm), (gl_in, glv, gl_hbm), (gr_in, grv, gr_hbm)]
    take = [pltpu.make_async_copy(ig_parts, ip, in_sem.at[0]), pltpu.make_async_copy(out_parts, op, in_sem.at[1])]
    take += [pltpu.make_async_copy(a, v, in_sem.at[2 + i]) for i, (a, v, _) in enumerate(passed)]
    give = [pltpu.make_async_copy(iv, ig_hbm, out_sem.at[0]), pltpu.make_async_copy(ov, out_hbm, out_sem.at[1])]
    give += [pltpu.make_async_copy(v, o, out_sem.at[2 + i]) for i, (_, v, o) in enumerate(passed)]
    for copy in take:
        copy.start()
    go_ref[...] = go_in[...]
    for parts, total, i in ((ip, iv, 0), (op, ov, 1)):
        take[i].wait()
        acc = parts[0].astype(F32)
        for o in range(1, parts.shape[0]):
            acc += parts[o].astype(F32)
        total[...] = acc.astype(BF16)[:own]
        give[i].start()
    for i in range(2, 5):
        take[i].wait()
        give[i].start()
    for copy in give:
        copy.wait()


def shards(
    hidden_in, out_grad, base_levels, base_scales, kron_outer, kron_left, kron_right,
    sparse_rows, sparse_cols, sparse_count, sparse_values,
):
    tile_rows, tile_cols = base_levels.shape
    slots, block = sparse_values.shape[2], sparse_values.shape[3]
    own = hidden_in.shape[0]
    pad = own + -own % 16
    rank = kron_left.shape[1]
    row_blocks, col_blocks = tile_rows // block, tile_cols // block
    n_d, n_c, n_t = lax.axis_size("dp"), lax.axis_size("sub"), lax.axis_size("tp")
    n_s = n_d * n_c
    full = n_s * pad
    kc = 4 * block if row_blocks % 4 == 0 else block
    fc = 4 * block if col_blocks % 4 == 0 else block
    nb, nf = tile_rows // kc, tile_cols // fc
    pieces = min(4, row_blocks)
    ks = window(row_blocks, n_s)[0]
    kt = window(ks, n_t)[0]
    rt = window(col_blocks, n_t)[0]
    rs = window(rt, n_s)[0]
    table_rows = -(-(row_blocks * col_blocks) // (8 * LANES)) * 8
    vmem = pl.BlockSpec(memory_space=pltpu.VMEM)
    smem = pl.BlockSpec(memory_space=pltpu.SMEM)
    any_ = pl.BlockSpec(memory_space=pl.ANY)
    dma = pltpu.SemaphoreType.DMA
    out_parts, ig_parts, go, gl, gr, gs = pl.pallas_call(
        functools.partial(kernel, (n_t, n_d, n_c, own, kc, fc, pieces)),
        in_specs=[smem] * 4 + [any_] * 7,
        out_specs=[any_, any_, vmem, any_, any_, any_],
        out_shape=[
            jax.ShapeDtypeStruct((n_t, pad, tile_cols), BF16),
            jax.ShapeDtypeStruct((n_d, pad, tile_rows), BF16),
            jax.ShapeDtypeStruct((1, 1), F32),
            jax.ShapeDtypeStruct((rank, tile_rows), F32),
            jax.ShapeDtypeStruct((rank, tile_cols), F32),
            jax.ShapeDtypeStruct((slots, block, block), F32),
        ],
        scratch_shapes=[
            pltpu.VMEM((tile_rows, tile_cols), BF16),
            pltpu.VMEM((n_s, own, tile_rows), BF16),
            pltpu.VMEM((row_blocks, full, block), BF16),
            pltpu.VMEM((n_t, own, tile_cols), BF16),
            pltpu.VMEM((col_blocks, full, block), BF16),
            pltpu.VMEM((rank, tile_rows), BF16),
            pltpu.VMEM((rank, tile_cols), BF16),
            pltpu.VMEM(base_scales.shape, BF16),
            pltpu.VMEM(base_scales.shape, F32),
            pltpu.VMEM((slots + 1, block, block), BF16),
            pltpu.VMEM((table_rows, LANES), jnp.int32),
            pltpu.SMEM((table_rows, LANES), jnp.int32),
            pltpu.VMEM((nb, n_c, n_d * pad, kc), BF16),
            pltpu.VMEM((nb, n_d * pad, kc), BF16),
            pltpu.VMEM((nb, n_d * pad, kc), BF16),
            pltpu.VMEM((nf, full, fc), BF16),
            pltpu.VMEM((full, rank), BF16),
            pltpu.VMEM((full, rank), BF16),
            pltpu.VMEM((n_s, rank, full), F32),
            pltpu.VMEM((n_t, rank, full), F32),
            pltpu.VMEM((rank, ks * LANES), BF16),
            pltpu.VMEM((n_t, rank, kt * LANES), BF16),
            pltpu.VMEM((rank, kt * LANES), BF16),
            pltpu.VMEM((n_t, rank, kt * LANES), BF16),
            pltpu.VMEM((rank, ks * LANES), BF16),
            pltpu.VMEM((n_s, rank, ks * LANES), BF16),
            pltpu.VMEM((rank, rt * LANES), F32),
            pltpu.VMEM((n_s, rank, rs * LANES), F32),
            pltpu.VMEM((rank, rs * LANES), F32),
            pltpu.VMEM((n_s, rank, rs * LANES), F32),
            pltpu.VMEM((rank, rt * LANES), F32),
            pltpu.VMEM((n_t, rank, rt * LANES), F32),
            pltpu.VMEM((rank, tile_rows), F32),
            pltpu.VMEM((rank, tile_cols), F32),
            pltpu.VMEM((slots, block, block), F32),
            dma((nb,)), dma((4,)), dma((1,)), dma((2,)),
            dma((n_d - 1, pieces)), dma((n_d - 1, pieces)), dma((n_d, pieces)), dma((n_d, pieces)),
            dma((n_t - 1,)), dma((n_t - 1,)),
            dma((nb,)), dma((nb,)), dma((n_d - 1, nb)), dma((n_d - 1, nb)), dma((nb,)),
            dma((n_t - 1, nf)), dma((n_t - 1, nf)), dma((nf,)),
            dma((n_s - 1,)), dma((n_s - 1,)), dma((n_t - 1,)), dma((n_t - 1,)),
            dma((n_t - 1,)), dma((n_t - 1,)), dma((n_t - 1,)), dma((n_t - 1,)), dma((n_s - 1,)), dma((n_s - 1,)),
            dma((n_s - 1,)), dma((n_s - 1,)), dma((n_s - 1,)), dma((n_s - 1,)), dma((n_t - 1,)), dma((n_t - 1,)),
            dma((3,)),
        ],
        compiler_params=pltpu.CompilerParams(
            vmem_limit_bytes=60 << 20, collective_id=0, has_side_effects=True
        ),
    )(
        sparse_rows, sparse_cols, sparse_count, kron_outer, hidden_in, out_grad, kron_left.T, kron_right,
        base_scales, sparse_values[0, 0], base_levels,
    )
    parts = [out_parts, ig_parts, go, gl, gr, gs]
    scratch = [pltpu.VMEM(p.shape, p.dtype) for p in parts]
    results = [
        jax.ShapeDtypeStruct((own, tile_cols), BF16), jax.ShapeDtypeStruct((own, tile_rows), BF16),
        *[jax.ShapeDtypeStruct(p.shape, p.dtype) for p in parts[2:]],
    ]
    layer_out, input_grad, go, gl, gr, gs = pl.pallas_call(
        finish,
        in_specs=[any_, any_, vmem, any_, any_, any_],
        out_specs=[any_, any_, vmem, any_, any_, any_],
        out_shape=results,
        scratch_shapes=[
            scratch[0], scratch[1], scratch[3], scratch[4], scratch[5],
            pltpu.VMEM((own, tile_cols), BF16), pltpu.VMEM((own, tile_rows), BF16), dma((5,)), dma((5,)),
        ],
        compiler_params=pltpu.CompilerParams(vmem_limit_bytes=60 << 20),
    )(*parts)
    return layer_out, input_grad, go, gl.T, gr, gs[None, None]


def solution(mesh):
    return jax.shard_map(
        shards,
        mesh=mesh,
        in_specs=(
            P(("grp", "dp", "sub"), "tp"),
            P(("grp", "tp"), ("dp", "sub")),
            P("tp", ("dp", "sub")),
            P("tp", ("dp", "sub")),
            P("tp", ("dp", "sub")),
            P(),
            P(),
            P("tp", ("dp", "sub"), None),
            P("tp", ("dp", "sub"), None),
            P("tp", ("dp", "sub")),
            P("tp", ("dp", "sub"), None, None, None),
        ),
        out_specs=(
            P(("grp", "tp"), ("dp", "sub")),
            P(("grp", "dp", "sub"), "tp"),
            P(("grp", "tp"), ("dp", "sub")),
            P("grp", None),
            P("grp", None),
            P(("grp", "tp"), ("dp", "sub"), None, None, None),
        ),
        check_vma=False,
    )
```
